32 devices in a mesh: dp: 8 (over z, x), seq: 4 (over y, core).
Axes of the slice: x: 2, y: 2, z: 4, core: 2. Of those that a mesh axis runs over, the one named last changes fastest.
Arguments:
- field: bfloat16 [8, 2048, 1024], P('dp', 'seq'), may hold values from -6 to 6
- eq_embed: bfloat16 [8, 512, 1024], P('dp', 'seq'), may hold values from -6 to 6
- eq_len: int32 [8], replicated, may hold values from 1 to 512, 2048 in all
- owner: int32 [8], replicated, may hold values from 0 to 7, as said below
- norm_gain: float32 [1024], replicated, may hold values from 0.1 to 1.9
- w_qkv: bfloat16 [1024, 3072], replicated, may hold values from -0.176776695 to 0.176776695
- w_out: bfloat16 [1024, 1024], replicated, may hold values from -0.1875 to 0.1875
- cross_gain: float32 [1024], replicated, may hold values from 0.1 to 1.9
- w_cq: bfloat16 [1024, 1024], replicated, may hold values from -0.125 to 0.125
- w_ckv: bfloat16 [1024, 2048], replicated, may hold values from -0.125 to 0.125
- w_cout: bfloat16 [1024, 1024], replicated, may hold values from -0.1875 to 0.1875
Outputs:
- joined: bfloat16 [8, 2048, 1024], P('dp', 'seq')
The draws below stay inside these ranges and needn't reach their ends.
Inputs may be any that keep to these rules, and one draw needn't show every extreme that they name: `owner`: every slot number appears exactly once. `eq_len`: some slot has all 512 tokens real.
All inputs are finite; a program needn't handle non-finite values.
Results may differ from the reference program's by a relative error of at most 0.0055.
Values may be sent and summed in bfloat16 or wider, within the bound.
A program may use at most 128 MiB of HBM per device.

```python
import math
import jax
import jax.numpy as jnp
import numpy as np
from jax import lax

D = 1024
HEADS = 16
HEAD_DIM = 64
EQ = 512
SEQ_LEN = 2048
SAMPLES = 8
N_DP = 8


def draw_owner(key, part):
    order_key = jax.random.fold_in(key, 11)
    pick_key = jax.random.fold_in(key, 12)
    order = jax.random.permutation(order_key, N_DP).astype(jnp.int32)
    chosen = jax.random.randint(pick_key, (), 0, N_DP, dtype=jnp.int32)
    target = (chosen + N_DP // 2) % N_DP
    holder = jnp.argmax((order == target).astype(jnp.int32)).astype(jnp.int32)
    previous = order[chosen]
    order = order.at[holder].set(previous)
    order = order.at[chosen].set(target)
    return order


def draw_w_qkv(key, part):
    weight_key = jax.random.fold_in(key, 21)
    columns = jnp.arange(3 * D, dtype=jnp.int32)
    column_scale = jnp.where(columns < 2 * D, (2.0 / D) ** 0.5, (1.0 / D) ** 0.5).astype(jnp.float32)
    base = jax.random.truncated_normal(weight_key, -4.0, 4.0, (D, 3 * D), jnp.float32)
    return (base * column_scale[None, :]).astype(jnp.bfloat16)


def block_scale(key, shape, cuts, low, largest):
    factor_of, own = 1.0, jax.random.fold_in(key, 6)
    for position, parts in cuts:
        steps = jnp.exp(jax.random.uniform(jax.random.fold_in(own, position), (parts,), jnp.float32, low / len(cuts), largest / len(cuts)))
        factor_of = factor_of * jnp.repeat(steps, shape[position] // parts).reshape([-1 if axis == position else 1 for axis in range(len(shape))])
    return factor_of


def split_up(amount, total, most, lean):
    portions = [(1 << 20) // math.isqrt(grade ** lean) + 1 for grade in range(2, amount + 1)]
    spare, given = total - most - (amount - 1), [1] * (amount - 1)
    while spare > 0:
        candidates = [i for i in range(amount - 1) if given[i] < most]
        whole, left = sum([portions[i] for i in candidates]), spare
        for i in candidates:
            more = min(most - given[i], max(1, left * portions[i] // whole), spare)
            given[i] = given[i] + more
            spare = spare - more
    return np.array([most] + given)


def uneven(stream_key, count, total, most, lean):
    if count == 2:
        one = jax.random.randint(stream_key, (), max(1, total - most), min(most, total - 1) + 1)
        return jnp.stack([one, total - one])
    lengths = jnp.asarray(split_up(count, total, most, lean), jnp.int32)
    pairs = (count - 1) // 2
    giver, sink = lengths[1:1 + 2 * pairs:2], lengths[2:2 + 2 * pairs:2]
    margin = jnp.minimum(giver - 1, most - sink)
    moved = jax.random.randint(jax.random.fold_in(stream_key, 1), (pairs,), 0, 1 << 20) % (margin + 1)
    lengths = lengths.at[1:1 + 2 * pairs:2].set(giver - moved).at[2:2 + 2 * pairs:2].set(sink + moved)
    return lengths[jax.random.permutation(jax.random.fold_in(stream_key, 2), count)]


def bell_draw(stream_key, dims, spread, bound, cuts=(), kind=jnp.bfloat16):
    array = jax.random.normal(stream_key, dims, jnp.float32) * spread
    if len(cuts) > 0:
        array = block_scale(stream_key, dims, cuts, -0.22, 0.18) * array
    return jnp.clip(array, min=-bound, max=bound).astype(kind)


def setup_inputs(seed: int = 0) -> dict:
    key_list = jax.random.split(jax.random.key(seed), 12)
    field = bell_draw(key_list[0], (SAMPLES, SEQ_LEN, D), 1.0, 6.0, ((0, 8), (1, 4)))
    eq_embed = bell_draw(key_list[1], (SAMPLES, EQ, D), 1.0, 6.0, ((0, 8), (1, 4)))
    eq_len = uneven(key_list[2], SAMPLES, N_DP * EQ // 2, EQ, 2).astype(jnp.int32)
    owner = draw_owner(jax.random.fold_in(key_list[11], 71), 0)
    norm_gain = jnp.clip(1.0 + 0.18 * jax.random.normal(key_list[4], (D,), jnp.float32), 0.1, 1.9)
    w_qkv = draw_w_qkv(jax.random.fold_in(key_list[11], 71), 0)
    w_out = bell_draw(key_list[6], (D, D), D ** -0.5, 0.1875)
    cross_gain = jnp.clip(1.0 + 0.18 * jax.random.normal(key_list[7], (D,), jnp.float32), 0.1, 1.9)
    w_cq = bell_draw(key_list[8], (D, D), (2 * D) ** -0.5, 0.125)
    w_ckv = bell_draw(key_list[9], (D, 2 * D), (2 * D) ** -0.5, 0.125)
    w_cout = bell_draw(key_list[10], (D, D), D ** -0.5, 0.1875)
    return {"field": field, "eq_embed": eq_embed, "eq_len": eq_len, "owner": owner, "norm_gain": norm_gain, "w_qkv": w_qkv, "w_out": w_out, "cross_gain": cross_gain, "w_cq": w_cq, "w_ckv": w_ckv, "w_cout": w_cout}


def normalize(values, gain):
    return values * lax.rsqrt(lax.optimization_barrier(jnp.mean(values * values, axis=-1, keepdims=True)) + 1e-06) * gain

def attend(query, keys, values, valid):
    rows = query.shape[0]
    heads = query.shape[1]
    depth = query.shape[2]
    block = min(512, rows)
    keys_f = keys.astype(jnp.float32)
    values_f = values.astype(jnp.float32)
    scale = depth ** (-0.5)

    def one_block(query_block):
        scores = jnp.einsum('qhd,khd->hqk', query_block.astype(jnp.float32), keys_f) * scale
        expo = jnp.where(valid[None, None, :], jnp.exp(scores), 0.0)
        weights = (expo / lax.optimization_barrier(jnp.sum(expo, axis=-1, keepdims=True))).astype(jnp.bfloat16)
        return jnp.einsum('hqk,khd->qhd', weights.astype(jnp.float32), values_f).astype(jnp.bfloat16)
    blocks = lax.map(one_block, query.reshape(rows // block, block, heads, depth))
    return blocks.reshape(rows, heads * depth)

def reference(field, eq_embed, eq_len, owner, norm_gain, w_qkv, w_out, cross_gain, w_cq, w_ckv, w_cout):

    def one_sample(index):
        tokens = field[index].astype(jnp.float32)
        normed = normalize(tokens, norm_gain).astype(jnp.bfloat16)
        projected = jnp.dot(normed, w_qkv, preferred_element_type=jnp.float32).astype(jnp.bfloat16)
        split = projected.reshape(SEQ_LEN, 3, HEADS, HEAD_DIM)
        every = jnp.ones((SEQ_LEN,), dtype=bool)
        attended = attend(split[:, 0], split[:, 1], split[:, 2], every)
        mixed = tokens + jnp.dot(attended, w_out, preferred_element_type=jnp.float32)
        cross_in = normalize(mixed, cross_gain).astype(jnp.bfloat16)
        cross_q = jnp.dot(cross_in, w_cq, preferred_element_type=jnp.float32).astype(jnp.bfloat16)
        slot = owner[index]
        equation = lax.dynamic_index_in_dim(eq_embed, slot, 0, keepdims=False)
        length = lax.dynamic_index_in_dim(eq_len, slot, 0, keepdims=False)
        eq_kv = jnp.dot(equation, w_ckv, preferred_element_type=jnp.float32).astype(jnp.bfloat16)
        eq_kv = eq_kv.reshape(EQ, 2, HEADS, HEAD_DIM)
        valid = jnp.arange(EQ, dtype=jnp.int32) < length
        cross_att = attend(cross_q.reshape(SEQ_LEN, HEADS, HEAD_DIM), eq_kv[:, 0], eq_kv[:, 1], valid)
        return (mixed + jnp.dot(cross_att, w_cout, preferred_element_type=jnp.float32)).astype(jnp.bfloat16)
    return lax.map(one_sample, jnp.arange(SAMPLES, dtype=jnp.int32))
```

```python
import functools
import math
import jax
import jax.numpy as jnp
from jax import lax
from jax.experimental import pallas as pl
from jax.experimental.pallas import tpu as pltpu
from jax.sharding import PartitionSpec as P

D = 1024
HEADS = 16
HEAD_DIM = 64
PAIR = 2 * HEAD_DIM
Q_SCALE = math.log2(math.e) * HEAD_DIM ** (-0.5)
V_SHRINK = 2.0 ** -10
V_GROW = 2.0 ** 10
CHUNKS = 2
MESH = pl.DeviceIdType.MESH


def rms(values, gain):
    return values * lax.rsqrt(jnp.mean(values * values, axis=-1, keepdims=True) + 1e-06) * gain


def dot(a, b):
    return jnp.dot(a, b, preferred_element_type=jnp.float32)


def dot_nt(a, b):
    return lax.dot_general(a, b, (((1,), (1,)), ((), ())), preferred_element_type=jnp.float32)


def low_lanes(rows):
    return lax.broadcasted_iota(jnp.int32, (rows, PAIR), 1) < HEAD_DIM


def finish(even, odd, low):
    total = pltpu.roll(jnp.where(low, odd, even), HEAD_DIM, axis=1)
    return (jnp.where(low, even, odd) * (V_GROW / total)).astype(jnp.bfloat16)


def self_kernel(
    x_ref, gain_ref, w_hbm, out_ref, xn, wbuf, q_s, k_s, v_s, acc, away,
    w_sem, part_send, part_recv, sib_send, sib_recv, fwd_send, fwd_recv, att_send, att_recv,
):
    me = lax.axis_index("seq")
    core = lax.rem(me, 2)
    sib = me + 1 - 2 * core
    part = lax.rem(me + 2, 4)
    rows = x_ref.shape[0]
    half = D // 2
    pairs = half // PAIR
    step = rows // CHUNKS

    loads = []
    for j in range(3):
        cols = pl.ds(pl.multiple_of(core * half + j * D, half), half)
        loads.append(pltpu.make_async_copy(w_hbm.at[:, cols], wbuf.at[j], w_sem.at[j]))
        loads[-1].start()
    barrier = pltpu.get_barrier_semaphore()
    for other in (sib, part):
        pl.semaphore_signal(barrier, inc=1, device_id={"seq": other}, device_id_type=MESH)
    gain = gain_ref[...]
    to_part, to_sib = [], []
    for i in range(CHUNKS):
        here = pl.ds(i * step, step)
        xn[0, here] = rms(x_ref[here].astype(jnp.float32), gain).astype(jnp.bfloat16)
        if i == 0:
            pl.semaphore_wait(barrier, 2)
        to_part.append(pltpu.make_async_remote_copy(
            src_ref=xn.at[0, here], dst_ref=xn.at[2, here],
            send_sem=part_send.at[i], recv_sem=part_recv.at[i],
            device_id={"seq": part}, device_id_type=MESH))
        to_part[-1].start()
        to_sib.append(pltpu.make_async_remote_copy(
            src_ref=xn.at[0, here], dst_ref=xn.at[1, here],
            send_sem=sib_send.at[i], recv_sem=sib_recv.at[i],
            device_id={"seq": sib}, device_id_type=MESH))
        to_sib[-1].start()
    for load in loads:
        load.wait()

    blk = 256
    low = low_lanes(blk)

    def project(slot, with_q):
        @pl.loop(0, rows // blk)
        def _(r):
            at = pl.ds(pl.multiple_of(r * blk, blk), blk)
            x = xn[slot, at]
            if with_q:
                qf = (dot(x, wbuf[0]) * Q_SCALE).astype(jnp.bfloat16)
                q_at = pl.ds(pl.multiple_of(slot * rows + r * blk, blk), blk)
                for p in range(pairs):
                    q_s[p, q_at] = qf[:, p * PAIR:(p + 1) * PAIR]
            kf = dot(x, wbuf[1])
            vf = dot(x, wbuf[2]) * V_SHRINK
            kv_at = pl.ds(pl.multiple_of(slot * rows + r * blk, blk), blk)
            for p in range(pairs):
                kp = kf[:, p * PAIR:(p + 1) * PAIR]
                vp = vf[:, p * PAIR:(p + 1) * PAIR]
                k_s[2 * p, kv_at] = jnp.where(low, kp, 0.0).astype(jnp.bfloat16)
                k_s[2 * p + 1, kv_at] = jnp.where(low, 0.0, kp).astype(jnp.bfloat16)
                v_s[2 * p, kv_at] = jnp.where(low, vp, 1.0).astype(jnp.bfloat16)
                v_s[2 * p + 1, kv_at] = jnp.where(low, 1.0, vp).astype(jnp.bfloat16)

    qblk = 512
    qlow = low_lanes(qblk)

    def piece(p, q_at, key_at):
        q = q_s[p, q_at]
        outs = []
        for h in range(2):
            w = jnp.exp2(dot_nt(q, k_s[2 * p + h, key_at])).astype(jnp.bfloat16)
            outs.append(dot(w, v_s[2 * p + h, key_at]))
        return outs

    project(0, True)
    for copy in to_sib:
        copy.wait_recv()
    project(1, True)

    @pl.loop(0, pairs * 2)
    def _(it):
        p = it // 2
        q_at = pl.ds(pl.multiple_of(lax.rem(it, 2) * qblk, qblk), qblk)
        for n in range(2):
            outs = piece(p, q_at, pl.ds(n * rows, rows))
            for h in range(2):
                if n == 0:
                    acc[2 * p + h, q_at] = outs[h]
                else:
                    acc[2 * p + h, q_at] += outs[h]

    for copy in to_part:
        copy.wait_recv()
    forwards = []
    for i in range(CHUNKS):
        here = pl.ds(i * step, step)
        forwards.append(pltpu.make_async_remote_copy(
            src_ref=xn.at[2, here], dst_ref=xn.at[3, here],
            send_sem=fwd_send.at[i], recv_sem=fwd_recv.at[i],
            device_id={"seq": sib}, device_id_type=MESH))
        forwards[-1].start()
    project(2, False)

    @pl.loop(0, pairs * 2)
    def _(it):
        p = it // 2
        q_at = pl.ds(pl.multiple_of(lax.rem(it, 2) * qblk, qblk), qblk)
        outs = piece(p, q_at, pl.ds(2 * rows, rows))
        for h in range(2):
            acc[2 * p + h, q_at] += outs[h]

    for copy in forwards:
        copy.wait_recv()
    project(3, False)

    def last(p, q_at):
        outs = piece(p, q_at, pl.ds(3 * rows, rows))
        even = acc[2 * p, q_at] + outs[0]
        odd = acc[2 * p + 1, q_at] + outs[1]
        return finish(even, odd, qlow)

    for p in range(pairs):
        away[:, p * PAIR:(p + 1) * PAIR] = last(p, pl.ds(rows, rows))
    back = pltpu.make_async_remote_copy(
        src_ref=away, dst_ref=out_ref.at[core], send_sem=att_send, recv_sem=att_recv,
        device_id={"seq": sib}, device_id_type=MESH)
    back.start()
    for p in range(pairs):
        out_ref[core, :, p * PAIR:(p + 1) * PAIR] = last(p, pl.ds(0, rows))
    back.wait()
    for copy in to_part + to_sib + forwards:
        copy.wait_send()


def self_attention(tokens, gain, w_qkv):
    rows = tokens.shape[0]
    half = D // 2
    vmem = pl.BlockSpec(memory_space=pltpu.VMEM)
    dma = pltpu.SemaphoreType.DMA
    return pl.pallas_call(
        self_kernel,
        name="self_attention",
        out_shape=jax.ShapeDtypeStruct((2, rows, half), jnp.bfloat16),
        in_specs=[vmem, vmem, pl.BlockSpec(memory_space=pl.ANY)],
        out_specs=vmem,
        scratch_shapes=[
            pltpu.VMEM((4, rows, D), jnp.bfloat16),
            pltpu.VMEM((3, D, half), jnp.bfloat16),
            pltpu.VMEM((half // PAIR, 2 * rows, PAIR), jnp.bfloat16),
            pltpu.VMEM((half // HEAD_DIM, 4 * rows, PAIR), jnp.bfloat16),
            pltpu.VMEM((half // HEAD_DIM, 4 * rows, PAIR), jnp.bfloat16),
            pltpu.VMEM((half // HEAD_DIM, 2 * rows, PAIR), jnp.float32),
            pltpu.VMEM((rows, half), jnp.bfloat16),
            dma((3,)),
            dma((CHUNKS,)), dma((CHUNKS,)), dma((CHUNKS,)), dma((CHUNKS,)),
            dma((CHUNKS,)), dma((CHUNKS,)), dma, dma,
        ],
        compiler_params=pltpu.CompilerParams(
            collective_id=0, has_side_effects=True, vmem_limit_bytes=50 << 20),
        cost_estimate=pl.CostEstimate(
            flops=14 * 10 ** 9, bytes_accessed=6 << 20, transcendentals=17 * 10 ** 6),
    )(tokens, gain.reshape(1, D), w_qkv)


def cross_kernel(
    len_ref, att_ref, x_ref, gain_ref, kv_ref, wo_hbm, wq_hbm, wc_hbm, out_ref,
    wo, wq, wc, q_s, mixed, att_s, w_sem,
):
    rows = x_ref.shape[0]
    keys = kv_ref.shape[0]
    half = D // 2
    loads = []
    for j, (src, dst) in enumerate(((wo_hbm, wo), (wq_hbm, wq), (wc_hbm, wc))):
        loads.append(pltpu.make_async_copy(src, dst, w_sem.at[j]))
        loads[-1].start()
    blk = 256
    loads[0].wait()
    loads[1].wait()

    @pl.loop(0, rows // blk)
    def _(r):
        at = pl.ds(pl.multiple_of(r * blk, blk), blk)
        m = (x_ref[at].astype(jnp.float32)
             + dot(att_ref[0, at], wo[:half]) + dot(att_ref[1, at], wo[half:]))
        mixed[at] = m
        cross_in = rms(m, gain_ref[...]).astype(jnp.bfloat16)
        qf = (dot(cross_in, wq[...]) * Q_SCALE).astype(jnp.bfloat16)
        for p in range(HEADS // 2):
            q_s[p, at] = qf[:, p * PAIR:(p + 1) * PAIR]

    low = low_lanes(keys)
    valid = lax.broadcasted_iota(jnp.int32, (keys, PAIR), 0) < len_ref[0]
    qlow = low_lanes(rows)
    one = jnp.where(valid, 1.0, 0.0)
    for p in range(HEADS // 2):
        cols = slice(p * PAIR, (p + 1) * PAIR)
        kp = jnp.where(valid, kv_ref[:, cols].astype(jnp.float32), 0.0)
        vp = jnp.where(valid, kv_ref[:, D + p * PAIR:D + (p + 1) * PAIR].astype(jnp.float32), 0.0)
        vp = vp * V_SHRINK
        q = q_s[p]
        outs = []
        for h in range(2):
            mine = low if h == 0 else jnp.logical_not(low)
            kh = jnp.where(mine, kp, 0.0).astype(jnp.bfloat16)
            vh = jnp.where(mine, vp, one).astype(jnp.bfloat16)
            w = jnp.exp2(dot_nt(q, kh)).astype(jnp.bfloat16)
            outs.append(dot(w, vh))
        att_s[:, cols] = finish(outs[0], outs[1], qlow)

    loads[2].wait()

    @pl.loop(0, rows // blk)
    def _(r):
        at = pl.ds(pl.multiple_of(r * blk, blk), blk)
        out_ref[at] = (mixed[at] + dot(att_s[at], wc[...])).astype(jnp.bfloat16)


def cross_attention(length, att, tokens, gain, kv, w_out, w_cq, w_cout):
    rows = tokens.shape[0]
    vmem = pl.BlockSpec(memory_space=pltpu.VMEM)
    hbm = pl.BlockSpec(memory_space=pl.ANY)
    return pl.pallas_call(
        cross_kernel,
        name="cross_attention",
        out_shape=jax.ShapeDtypeStruct((rows, D), jnp.bfloat16),
        in_specs=[pl.BlockSpec(memory_space=pltpu.SMEM), vmem, vmem, vmem, vmem, hbm, hbm, hbm],
        out_specs=vmem,
        scratch_shapes=[
            pltpu.VMEM((D, D), jnp.bfloat16),
            pltpu.VMEM((D, D), jnp.bfloat16),
            pltpu.VMEM((D, D), jnp.bfloat16),
            pltpu.VMEM((HEADS // 2, rows, PAIR), jnp.bfloat16),
            pltpu.VMEM((rows, D), jnp.float32),
            pltpu.VMEM((rows, D), jnp.bfloat16),
            pltpu.SemaphoreType.DMA((3,)),
        ],
        compiler_params=pltpu.CompilerParams(vmem_limit_bytes=40 << 20),
        cost_estimate=pl.CostEstimate(
            flops=6 * 10 ** 9, bytes_accessed=12 << 20, transcendentals=4 * 10 ** 6),
    )(length, att, tokens, gain.reshape(1, D), kv, w_out, w_cq, w_cout)


def per_device(
    field, eq_embed, eq_len, owner, norm_gain, w_qkv, w_out, cross_gain, w_cq, w_ckv, w_cout
):
    tokens = field[0]
    slot = lax.dynamic_index_in_dim(owner, lax.axis_index("dp"), 0, keepdims=False)
    length = lax.dynamic_slice_in_dim(eq_len, slot, 1, 0)
    slots = lax.all_gather(eq_embed, "dp", axis=0, tiled=True)
    att = self_attention(tokens, norm_gain, w_qkv)
    owned = lax.dynamic_index_in_dim(slots, slot, 0, keepdims=False)
    equation = lax.all_gather(owned, "seq", axis=0, tiled=True)
    kv = jnp.dot(equation, w_ckv, preferred_element_type=jnp.float32).astype(jnp.bfloat16)
    return cross_attention(length, att, tokens, cross_gain, kv, w_out, w_cq, w_cout)[None]


def solution(mesh):
    split = P("dp", "seq", None)
    in_specs = (split, split) + (P(),) * 9
    return jax.shard_map(
        per_device, mesh=mesh, in_specs=in_specs, out_specs=split, check_vma=False
    )
```

```python
import functools
import math
import jax
import jax.numpy as jnp
from jax import lax
from jax.experimental import pallas as pl
from jax.experimental.pallas import tpu as pltpu
from jax.sharding import PartitionSpec as P

D = 1024
HEADS = 16
HEAD_DIM = 64
PAIR = 2 * HEAD_DIM
Q_SCALE = math.log2(math.e) * HEAD_DIM ** (-0.5)
V_SHRINK = 2.0 ** -10
V_GROW = 2.0 ** 10
CHUNKS = 2
MESH = pl.DeviceIdType.MESH


def rms(values, gain):
    return values * lax.rsqrt(jnp.mean(values * values, axis=-1, keepdims=True) + 1e-06) * gain


def dot(a, b):
    return jnp.dot(a, b, preferred_element_type=jnp.float32)


def dot_nt(a, b):
    return lax.dot_general(a, b, (((1,), (1,)), ((), ())), preferred_element_type=jnp.float32)


def low_lanes(rows):
    return lax.broadcasted_iota(jnp.int32, (rows, PAIR), 1) < HEAD_DIM


def finish(even, odd, low):
    total = pltpu.roll(jnp.where(low, odd, even), HEAD_DIM, axis=1)
    return (jnp.where(low, even, odd) * (V_GROW / total)).astype(jnp.bfloat16)


def self_kernel(
    owner_ref, x_ref, gain_ref, eq_ref, w_hbm, out_ref, eq_out,
    xn, wbuf, q_s, k_s, v_s, acc, away, got, picked,
    w_sem, part_send, part_recv, sib_send, sib_recv, fwd_send, fwd_recv, att_send, att_recv,
    one_send, one_recv, two_send, two_recv, eq_send, eq_recv,
):
    slots = eq_ref.shape[0]
    my_dp = lax.axis_index("dp")
    me = lax.axis_index("seq")
    core = lax.rem(me, 2)
    sib = me + 1 - 2 * core
    part = lax.rem(me + 2, 4)
    rows = x_ref.shape[0]
    half = D // 2
    pairs = half // PAIR
    step = rows // CHUNKS

    loads = []
    for j in range(3):
        cols = pl.ds(pl.multiple_of(core * half + j * D, half), half)
        loads.append(pltpu.make_async_copy(w_hbm.at[:, cols], wbuf.at[j], w_sem.at[j]))
        loads[-1].start()
    barrier = pltpu.get_barrier_semaphore()
    for other in (sib, part):
        pl.semaphore_signal(barrier, inc=1, device_id={"seq": other}, device_id_type=MESH)

    @pl.loop(1, slots)
    def _(i):
        peer = lax.rem(my_dp + i, slots)
        pl.semaphore_signal(barrier, inc=1, device_id={"dp": peer}, device_id_type=MESH)

    def scatter(i):
        peer = lax.rem(my_dp + i, slots)
        return pltpu.make_async_remote_copy(
            src_ref=eq_ref.at[peer], dst_ref=got.at[my_dp],
            send_sem=one_send.at[i], recv_sem=one_recv.at[i],
            device_id={"dp": peer}, device_id_type=MESH)

    def deliver(i):
        peer = lax.rem(my_dp + i, slots)
        return pltpu.make_async_remote_copy(
            src_ref=picked.at[i], dst_ref=eq_out.at[me, my_dp],
            send_sem=two_send.at[i], recv_sem=two_recv.at[i],
            device_id={"dp": peer}, device_id_type=MESH)

    gain = gain_ref[...]
    to_part, to_sib = [], []
    for i in range(CHUNKS):
        here = pl.ds(i * step, step)
        xn[0, here] = rms(x_ref[here].astype(jnp.float32), gain).astype(jnp.bfloat16)
        if i == 0:
            pl.semaphore_wait(barrier, slots + 1)
        to_part.append(pltpu.make_async_remote_copy(
            src_ref=xn.at[0, here], dst_ref=xn.at[2, here],
            send_sem=part_send.at[i], recv_sem=part_recv.at[i],
            device_id={"seq": part}, device_id_type=MESH))
        to_part[-1].start()
        to_sib.append(pltpu.make_async_remote_copy(
            src_ref=xn.at[0, here], dst_ref=xn.at[1, here],
            send_sem=sib_send.at[i], recv_sem=sib_recv.at[i],
            device_id={"seq": sib}, device_id_type=MESH))
        to_sib[-1].start()

    @pl.loop(1, slots)
    def _(i):
        scatter(i).start()

    got[my_dp] = eq_ref[my_dp]
    for load in loads:
        load.wait()

    blk = 256
    low = low_lanes(blk)

    def project(slot, with_q):
        @pl.loop(0, rows // blk)
        def _(r):
            at = pl.ds(pl.multiple_of(r * blk, blk), blk)
            x = xn[slot, at]
            if with_q:
                qf = (dot(x, wbuf[0]) * Q_SCALE).astype(jnp.bfloat16)
                q_at = pl.ds(pl.multiple_of(slot * rows + r * blk, blk), blk)
                for p in range(pairs):
                    q_s[p, q_at] = qf[:, p * PAIR:(p + 1) * PAIR]
            kf = dot(x, wbuf[1])
            vf = dot(x, wbuf[2]) * V_SHRINK
            kv_at = pl.ds(pl.multiple_of(slot * rows + r * blk, blk), blk)
            for p in range(pairs):
                kp = kf[:, p * PAIR:(p + 1) * PAIR]
                vp = vf[:, p * PAIR:(p + 1) * PAIR]
                k_s[2 * p, kv_at] = jnp.where(low, kp, 0.0).astype(jnp.bfloat16)
                k_s[2 * p + 1, kv_at] = jnp.where(low, 0.0, kp).astype(jnp.bfloat16)
                v_s[2 * p, kv_at] = jnp.where(low, vp, 1.0).astype(jnp.bfloat16)
                v_s[2 * p + 1, kv_at] = jnp.where(low, 1.0, vp).astype(jnp.bfloat16)

    qblk = 512
    qlow = low_lanes(qblk)

    def piece(p, q_at, key_at):
        q = q_s[p, q_at]
        outs = []
        for h in range(2):
            w = jnp.exp2(dot_nt(q, k_s[2 * p + h, key_at])).astype(jnp.bfloat16)
            outs.append(dot(w, v_s[2 * p + h, key_at]))
        return outs

    project(0, True)

    @pl.loop(1, slots)
    def _(i):
        scatter(i).wait()

    @pl.loop(1, slots)
    def _(i):
        picked[i] = got[owner_ref[lax.rem(my_dp + i, slots)]]
        deliver(i).start()

    eq_out[me, my_dp] = got[owner_ref[my_dp]]
    for copy in to_sib:
        copy.wait_recv()
    project(1, True)

    def local(it):
        p = it // 2
        q_at = pl.ds(pl.multiple_of(lax.rem(it, 2) * qblk, qblk), qblk)
        for n in range(2):
            outs = piece(p, q_at, pl.ds(n * rows, rows))
            for h in range(2):
                if n == 0:
                    acc[2 * p + h, q_at] = outs[h]
                else:
                    acc[2 * p + h, q_at] += outs[h]

    pl.loop(0, pairs)(local)

    @pl.loop(1, slots)
    def _(i):
        deliver(i).wait()

    eq_part = pltpu.make_async_remote_copy(
        src_ref=eq_out.at[me], dst_ref=eq_out.at[me],
        send_sem=eq_send.at[0], recv_sem=eq_recv.at[0],
        device_id={"seq": part}, device_id_type=MESH)
    eq_part.start()
    eq_sib = pltpu.make_async_remote_copy(
        src_ref=eq_out.at[me], dst_ref=eq_out.at[me],
        send_sem=eq_send.at[1], recv_sem=eq_recv.at[1],
        device_id={"seq": sib}, device_id_type=MESH)
    eq_sib.start()
    pl.loop(pairs, pairs * 2)(local)

    for copy in to_part:
        copy.wait_recv()
    forwards = []
    for i in range(CHUNKS):
        here = pl.ds(i * step, step)
        forwards.append(pltpu.make_async_remote_copy(
            src_ref=xn.at[2, here], dst_ref=xn.at[3, here],
            send_sem=fwd_send.at[i], recv_sem=fwd_recv.at[i],
            device_id={"seq": sib}, device_id_type=MESH))
        forwards[-1].start()
    eq_part.wait_recv()
    eq_fwd = pltpu.make_async_remote_copy(
        src_ref=eq_out.at[part], dst_ref=eq_out.at[part],
        send_sem=eq_send.at[2], recv_sem=eq_recv.at[2],
        device_id={"seq": sib}, device_id_type=MESH)
    eq_fwd.start()
    project(2, False)

    @pl.loop(0, pairs * 2)
    def _(it):
        p = it // 2
        q_at = pl.ds(pl.multiple_of(lax.rem(it, 2) * qblk, qblk), qblk)
        outs = piece(p, q_at, pl.ds(2 * rows, rows))
        for h in range(2):
            acc[2 * p + h, q_at] += outs[h]

    for copy in forwards:
        copy.wait_recv()
    project(3, False)

    def last(p, q_at):
        outs = piece(p, q_at, pl.ds(3 * rows, rows))
        even = acc[2 * p, q_at] + outs[0]
        odd = acc[2 * p + 1, q_at] + outs[1]
        return finish(even, odd, qlow)

    for p in range(pairs):
        away[:, p * PAIR:(p + 1) * PAIR] = last(p, pl.ds(rows, rows))
    back = pltpu.make_async_remote_copy(
        src_ref=away, dst_ref=out_ref.at[core], send_sem=att_send, recv_sem=att_recv,
        device_id={"seq": sib}, device_id_type=MESH)
    back.start()
    for p in range(pairs):
        out_ref[core, :, p * PAIR:(p + 1) * PAIR] = last(p, pl.ds(0, rows))
    back.wait()
    eq_part.wait_send()
    eq_sib.wait()
    eq_fwd.wait()
    for copy in to_part + to_sib + forwards:
        copy.wait_send()


def self_attention(owner, tokens, gain, eq, w_qkv):
    rows = tokens.shape[0]
    slots = owner.shape[0]
    pieces = eq.reshape(slots, eq.shape[0] // slots, D)
    half = D // 2
    vmem = pl.BlockSpec(memory_space=pltpu.VMEM)
    dma = pltpu.SemaphoreType.DMA
    return pl.pallas_call(
        self_kernel,
        name="self_attention",
        out_shape=(
            jax.ShapeDtypeStruct((2, rows, half), jnp.bfloat16),
            jax.ShapeDtypeStruct((4,) + pieces.shape, jnp.bfloat16),
        ),
        in_specs=[
            pl.BlockSpec(memory_space=pltpu.SMEM), vmem, vmem, vmem,
            pl.BlockSpec(memory_space=pltpu.HBM),
        ],
        out_specs=(vmem, vmem),
        scratch_shapes=[
            pltpu.VMEM((4, rows, D), jnp.bfloat16),
            pltpu.VMEM((3, D, half), jnp.bfloat16),
            pltpu.VMEM((half // PAIR, 2 * rows, PAIR), jnp.bfloat16),
            pltpu.VMEM((half // HEAD_DIM, 4 * rows, PAIR), jnp.bfloat16),
            pltpu.VMEM((half // HEAD_DIM, 4 * rows, PAIR), jnp.bfloat16),
            pltpu.VMEM((half // HEAD_DIM, 2 * rows, PAIR), jnp.float32),
            pltpu.VMEM((rows, half), jnp.bfloat16),
            pltpu.VMEM(pieces.shape, jnp.bfloat16),
            pltpu.VMEM(pieces.shape, jnp.bfloat16),
            dma((3,)),
            dma((CHUNKS,)), dma((CHUNKS,)), dma((CHUNKS,)), dma((CHUNKS,)),
            dma((CHUNKS,)), dma((CHUNKS,)), dma, dma,
            dma((slots,)), dma((slots,)), dma((slots,)), dma((slots,)), dma((3,)), dma((3,)),
        ],
        compiler_params=pltpu.CompilerParams(
            collective_id=0, has_side_effects=True, vmem_limit_bytes=32 << 20),
        cost_estimate=pl.CostEstimate(
            flops=14 * 10 ** 9, bytes_accessed=6 << 20, transcendentals=17 * 10 ** 6),
    )(owner, tokens, gain.reshape(1, D), pieces, w_qkv)


def cross_kernel(
    len_ref, owner_ref, att_ref, x_ref, gain_ref, eq_ref, wo, wq, wkv, wc, out_ref,
    q_s, kv_ref, mixed, att_s,
):
    rows = x_ref.shape[0]
    keys = eq_ref.shape[0]
    half = D // 2
    blk = 256
    for j in range(4):
        cols = slice(j * half, (j + 1) * half)
        kv_ref[:, cols] = dot(eq_ref[...], wkv[:, cols]).astype(jnp.bfloat16)

    @pl.loop(0, rows // blk)
    def _(r):
        at = pl.ds(pl.multiple_of(r * blk, blk), blk)
        m = (x_ref[at].astype(jnp.float32)
             + dot(att_ref[0, at], wo[:half]) + dot(att_ref[1, at], wo[half:]))
        mixed[at] = m
        cross_in = rms(m, gain_ref[...]).astype(jnp.bfloat16)
        qf = (dot(cross_in, wq[...]) * Q_SCALE).astype(jnp.bfloat16)
        for p in range(HEADS // 2):
            q_s[p, at] = qf[:, p * PAIR:(p + 1) * PAIR]

    length = len_ref[owner_ref[lax.axis_index("dp")]]
    low = low_lanes(keys)
    valid = lax.broadcasted_iota(jnp.int32, (keys, PAIR), 0) < length
    qlow = low_lanes(rows)
    one = jnp.where(valid, 1.0, 0.0)
    for p in range(HEADS // 2):
        cols = slice(p * PAIR, (p + 1) * PAIR)
        kp = jnp.where(valid, kv_ref[:, cols].astype(jnp.float32), 0.0)
        vp = jnp.where(valid, kv_ref[:, D + p * PAIR:D + (p + 1) * PAIR].astype(jnp.float32), 0.0)
        vp = vp * V_SHRINK
        q = q_s[p]
        outs = []
        for h in range(2):
            mine = low if h == 0 else jnp.logical_not(low)
            kh = jnp.where(mine, kp, 0.0).astype(jnp.bfloat16)
            vh = jnp.where(mine, vp, one).astype(jnp.bfloat16)
            w = jnp.exp2(dot_nt(q, kh)).astype(jnp.bfloat16)
            outs.append(dot(w, vh))
        att_s[:, cols] = finish(outs[0], outs[1], qlow)

    @pl.loop(0, rows // blk)
    def _(r):
        at = pl.ds(pl.multiple_of(r * blk, blk), blk)
        out_ref[at] = (mixed[at] + dot(att_s[at], wc[...])).astype(jnp.bfloat16)


def cross_attention(eq_len, owner, att, tokens, gain, eq, w_out, w_cq, w_ckv, w_cout):
    rows = tokens.shape[0]
    vmem = pl.BlockSpec(memory_space=pltpu.VMEM)
    return pl.pallas_call(
        cross_kernel,
        name="cross_attention",
        out_shape=jax.ShapeDtypeStruct((rows, D), jnp.bfloat16),
        in_specs=[pl.BlockSpec(memory_space=pltpu.SMEM)] * 2 + [vmem] * 8,
        out_specs=vmem,
        scratch_shapes=[
            pltpu.VMEM((HEADS // 2, rows, PAIR), jnp.bfloat16),
            pltpu.VMEM((eq.shape[0], 2 * D), jnp.bfloat16),
            pltpu.VMEM((rows, D), jnp.float32),
            pltpu.VMEM((rows, D), jnp.bfloat16),
        ],
        compiler_params=pltpu.CompilerParams(vmem_limit_bytes=40 << 20),
        cost_estimate=pl.CostEstimate(
            flops=6 * 10 ** 9, bytes_accessed=12 << 20, transcendentals=4 * 10 ** 6),
    )(eq_len, owner, att, tokens, gain.reshape(1, D), eq, w_out, w_cq, w_ckv, w_cout)


def per_device(
    field, eq_embed, eq_len, owner, norm_gain, w_qkv, w_out, cross_gain, w_cq, w_ckv, w_cout
):
    tokens = field[0]
    att, eq = self_attention(owner, tokens, norm_gain, eq_embed[0], w_qkv)
    return cross_attention(
        eq_len, owner, att, tokens, cross_gain, eq.reshape(-1, D), w_out, w_cq, w_ckv, w_cout)[None]


def solution(mesh):
    split = P("dp", "seq", None)
    in_specs = (split, split) + (P(),) * 9
    return jax.shard_map(
        per_device, mesh=mesh, in_specs=in_specs, out_specs=split, check_vma=False
    )
```

```python
import math
import jax
import jax.numpy as jnp
from jax import lax
from jax.experimental import pallas as pl
from jax.experimental.pallas import tpu as pltpu
from jax.sharding import PartitionSpec as P

D = 1024
HEADS = 16
HEAD_DIM = 64
PAIR = 2 * HEAD_DIM
Q_SCALE = math.log2(math.e) * HEAD_DIM ** (-0.5)
V_SHRINK = 2.0 ** -10
V_GROW = 2.0 ** 10
CHUNKS = 2
MESH = pl.DeviceIdType.MESH


def rms(values, gain):
    return values * lax.rsqrt(jnp.mean(values * values, axis=-1, keepdims=True) + 1e-06) * gain


def dot(a, b):
    return jnp.dot(a, b, preferred_element_type=jnp.float32)


def dot_nt(a, b):
    return lax.dot_general(a, b, (((1,), (1,)), ((), ())), preferred_element_type=jnp.float32)


def low_lanes(rows):
    return lax.broadcasted_iota(jnp.int32, (rows, PAIR), 1) < HEAD_DIM


def finish(even, odd, low):
    total = pltpu.roll(jnp.where(low, odd, even), HEAD_DIM, axis=1)
    return (jnp.where(low, even, odd) * (V_GROW / total)).astype(jnp.bfloat16)


def kernel(
    owner_ref, len_ref, x_hbm, gain_hbm, cross_gain_hbm, eq_hbm,
    w_hbm, wo_hbm, wq_hbm, wkv_hbm, wc_hbm, out_ref,
    x_ref, gains, eq_ref, wbuf, wo, wq, wkv, wc,
    xn, q_s, k_s, v_s, acc, away, att, got, picked, eq_out, cross_q, kv_s, mixed, cross_att,
    x_sem, g_sem, e_sem, w_sem,
    part_send, part_recv, sib_send, sib_recv, fwd_send, fwd_recv, att_send, att_recv,
    one_send, one_recv, two_send, two_recv, eq_send, eq_recv,
):
    slots = eq_ref.shape[0]
    my_dp = lax.axis_index("dp")
    me = lax.axis_index("seq")
    core = lax.rem(me, 2)
    sib = me + 1 - 2 * core
    part = lax.rem(me + 2, 4)
    rows = x_ref.shape[0]
    half = D // 2
    pairs = half // PAIR
    step = rows // CHUNKS

    def load(src, dst, sem):
        copy = pltpu.make_async_copy(src, dst, sem)
        copy.start()
        return copy

    x_loads = []
    for i in range(CHUNKS):
        here = pl.ds(i * step, step)
        x_loads.append(load(x_hbm.at[here], x_ref.at[here], x_sem.at[i]))
        if i == 0:
            gain_load = load(gain_hbm, gains.at[0], g_sem.at[0])
    eq_load = load(eq_hbm, eq_ref, e_sem)
    w_loads = []
    for j in range(3):
        cols = pl.ds(pl.multiple_of(core * half + j * D, half), half)
        w_loads.append(load(w_hbm.at[:, cols], wbuf.at[j], w_sem.at[j]))
    cross_gain_load = load(cross_gain_hbm, gains.at[1], g_sem.at[1])
    late = [
        load(src, dst, w_sem.at[3 + j])
        for j, (src, dst) in enumerate(((wkv_hbm, wkv), (wo_hbm, wo), (wq_hbm, wq), (wc_hbm, wc)))
    ]

    barrier = pltpu.get_barrier_semaphore()
    for other in (sib, part):
        pl.semaphore_signal(barrier, inc=1, device_id={"seq": other}, device_id_type=MESH)

    @pl.loop(1, slots)
    def _(i):
        peer = lax.rem(my_dp + i, slots)
        pl.semaphore_signal(barrier, inc=1, device_id={"dp": peer}, device_id_type=MESH)

    def scatter(i):
        peer = lax.rem(my_dp + i, slots)
        return pltpu.make_async_remote_copy(
            src_ref=eq_ref.at[peer], dst_ref=got.at[my_dp],
            send_sem=one_send.at[i], recv_sem=one_recv.at[i],
            device_id={"dp": peer}, device_id_type=MESH)

    def deliver(i):
        peer = lax.rem(my_dp + i, slots)
        return pltpu.make_async_remote_copy(
            src_ref=picked.at[i], dst_ref=eq_out.at[me, my_dp],
            send_sem=two_send.at[i], recv_sem=two_recv.at[i],
            device_id={"dp": peer}, device_id_type=MESH)

    def push(src, dst, send, recv, other):
        copy = pltpu.make_async_remote_copy(
            src_ref=src, dst_ref=dst, send_sem=send, recv_sem=recv,
            device_id={"seq": other}, device_id_type=MESH)
        copy.start()
        return copy

    gain_load.wait()
    gain = gains[0]
    to_part, to_sib = [], []
    for i in range(CHUNKS):
        here = pl.ds(i * step, step)
        x_loads[i].wait()
        xn[0, here] = rms(x_ref[here].astype(jnp.float32), gain).astype(jnp.bfloat16)
        if i == 0:
            pl.semaphore_wait(barrier, slots + 1)
        to_part.append(
            push(xn.at[0, here], xn.at[2, here], part_send.at[i], part_recv.at[i], part))
        to_sib.append(
            push(xn.at[0, here], xn.at[1, here], sib_send.at[i], sib_recv.at[i], sib))
    eq_load.wait()

    @pl.loop(1, slots)
    def _(i):
        scatter(i).start()

    got[my_dp] = eq_ref[my_dp]
    for copy in w_loads:
        copy.wait()

    low = low_lanes(step)

    def project(slot, i, with_q):
        at = pl.ds(i * step, step)
        x = xn[slot, at]
        key_at = pl.ds(slot * rows + i * step, step)
        if with_q:
            qf = (dot(x, wbuf[0]) * Q_SCALE).astype(jnp.bfloat16)
            for p in range(pairs):
                q_s[p, key_at] = qf[:, p * PAIR:(p + 1) * PAIR]
        kf = dot(x, wbuf[1])
        vf = dot(x, wbuf[2]) * V_SHRINK
        for p in range(pairs):
            kp = kf[:, p * PAIR:(p + 1) * PAIR]
            vp = vf[:, p * PAIR:(p + 1) * PAIR]
            k_s[2 * p, key_at] = jnp.where(low, kp, 0.0).astype(jnp.bfloat16)
            k_s[2 * p + 1, key_at] = jnp.where(low, 0.0, kp).astype(jnp.bfloat16)
            v_s[2 * p, key_at] = jnp.where(low, vp, 1.0).astype(jnp.bfloat16)
            v_s[2 * p + 1, key_at] = jnp.where(low, 1.0, vp).astype(jnp.bfloat16)

    def piece(p, h, q_at, key_at):
        w = jnp.exp2(dot_nt(q_s[p, q_at], k_s[2 * p + h, key_at])).astype(jnp.bfloat16)
        return dot(w, v_s[2 * p + h, key_at])

    every = pl.ds(0, 2 * rows)

    for i in range(CHUNKS):
        project(0, i, True)

    @pl.loop(1, slots)
    def _(i):
        scatter(i).wait()

    @pl.loop(1, slots)
    def _(i):
        picked[i] = got[owner_ref[lax.rem(my_dp + i, slots)]]
        deliver(i).start()

    eq_out[me, my_dp] = got[owner_ref[my_dp]]
    for i in range(CHUNKS):
        to_sib[i].wait_recv()
        project(1, i, True)

    def local(p):
        for h in range(2):
            acc[2 * p + h] = piece(p, h, every, pl.ds(0, rows))
        for h in range(2):
            acc[2 * p + h] += piece(p, h, every, pl.ds(rows, rows))

    pl.loop(0, pairs // 2)(local)

    @pl.loop(1, slots)
    def _(i):
        deliver(i).wait()

    mine = eq_out.at[me]
    eq_part = push(mine, mine, eq_send.at[0], eq_recv.at[0], part)
    eq_sib = push(mine, mine, eq_send.at[1], eq_recv.at[1], sib)
    pl.loop(pairs // 2, pairs)(local)

    forwards = []
    for i in range(CHUNKS):
        here = pl.ds(i * step, step)
        to_part[i].wait_recv()
        forwards.append(
            push(xn.at[2, here], xn.at[3, here], fwd_send.at[i], fwd_recv.at[i], sib))
        for slot in (2, 3):
            if slot == 3:
                if i == CHUNKS - 1:
                    eq_part.wait_recv()
                    theirs = eq_out.at[part]
                    eq_fwd = push(theirs, theirs, eq_send.at[2], eq_recv.at[2], sib)
                forwards[i].wait_recv()
            project(slot, i, False)
            key_at = pl.ds(slot * rows + i * step, step)
            if slot == 3 and i == CHUNKS - 1:
                break

            @pl.loop(0, pairs)
            def _(p):
                for h in range(2):
                    acc[2 * p + h] += piece(p, h, every, key_at)

    qlow = low_lanes(rows)

    def last(p, q_at):
        even = acc[2 * p, q_at] + piece(p, 0, q_at, key_at)
        odd = acc[2 * p + 1, q_at] + piece(p, 1, q_at, key_at)
        return finish(even, odd, qlow)

    for p in range(pairs):
        away[:, p * PAIR:(p + 1) * PAIR] = last(p, pl.ds(rows, rows))
    back = push(away, att.at[core], att_send, att_recv, sib)
    for p in range(pairs):
        att[core, :, p * PAIR:(p + 1) * PAIR] = last(p, pl.ds(0, rows))

    eq_part.wait_send()
    eq_sib.wait()
    eq_fwd.wait()
    cross_gain_load.wait()
    for copy in late:
        copy.wait()
    keys = kv_s.shape[0]
    equation = eq_out[...].reshape(keys, D)
    for j in range(4):
        cols = slice(j * half, (j + 1) * half)
        kv_s[:, cols] = dot(equation, wkv[:, cols]).astype(jnp.bfloat16)
    back.wait()
    for copy in to_part + to_sib + forwards:
        copy.wait_send()

    @pl.loop(0, CHUNKS)
    def _(r):
        at = pl.ds(pl.multiple_of(r * step, step), step)
        m = (x_ref[at].astype(jnp.float32)
             + dot(att[0, at], wo[:half]) + dot(att[1, at], wo[half:]))
        mixed[at] = m
        cross_in = rms(m, gains[1]).astype(jnp.bfloat16)
        qf = (dot(cross_in, wq[...]) * Q_SCALE).astype(jnp.bfloat16)
        for p in range(HEADS // 2):
            cross_q[p, at] = qf[:, p * PAIR:(p + 1) * PAIR]

    length = len_ref[owner_ref[my_dp]]
    klow = low_lanes(keys)
    valid = lax.broadcasted_iota(jnp.int32, (keys, PAIR), 0) < length
    one = jnp.where(valid, 1.0, 0.0)
    for p in range(HEADS // 2):
        cols = slice(p * PAIR, (p + 1) * PAIR)
        kp = jnp.where(valid, kv_s[:, cols].astype(jnp.float32), 0.0)
        vp = jnp.where(valid, kv_s[:, D + p * PAIR:D + (p + 1) * PAIR].astype(jnp.float32), 0.0)
        vp = vp * V_SHRINK
        outs = []
        for h in range(2):
            own = klow if h == 0 else jnp.logical_not(klow)
            kh = jnp.where(own, kp, 0.0).astype(jnp.bfloat16)
            vh = jnp.where(own, vp, one).astype(jnp.bfloat16)
            w = jnp.exp2(dot_nt(cross_q[p], kh)).astype(jnp.bfloat16)
            outs.append(dot(w, vh))
        cross_att[:, cols] = finish(outs[0], outs[1], qlow)

    @pl.loop(0, CHUNKS)
    def _(r):
        at = pl.ds(pl.multiple_of(r * step, step), step)
        out_ref[at] = (mixed[at] + dot(cross_att[at], wc[...])).astype(jnp.bfloat16)


def per_device(
    field, eq_embed, eq_len, owner, norm_gain, w_qkv, w_out, cross_gain, w_cq, w_ckv, w_cout
):
    tokens = field[0]
    rows = tokens.shape[0]
    half = D // 2
    slots = owner.shape[0]
    pieces = eq_embed.reshape(slots, eq_embed.shape[1] // slots, D)
    groups = lax.axis_size("seq")
    keys = groups * eq_embed.shape[1]
    any_space = pl.BlockSpec(memory_space=pl.ANY)
    smem = pl.BlockSpec(memory_space=pltpu.SMEM)
    dma = pltpu.SemaphoreType.DMA
    bf16 = lambda *shape: pltpu.VMEM(shape, jnp.bfloat16)
    f32 = lambda *shape: pltpu.VMEM(shape, jnp.float32)
    chunk_sem = dma((CHUNKS,))
    slot_sem = dma((slots,))
    joined = pl.pallas_call(
        kernel,
        name="joining_layer",
        out_shape=jax.ShapeDtypeStruct((rows, D), jnp.bfloat16),
        in_specs=[smem] * 2 + [any_space] * 9,
        out_specs=pl.BlockSpec(memory_space=pltpu.VMEM),
        scratch_shapes=[
            bf16(rows, D), f32(2, 1, D), bf16(*pieces.shape), bf16(3, D, half),
            bf16(D, D), bf16(D, D), bf16(D, 2 * D), bf16(D, D),
            bf16(groups, rows, D),
            bf16(half // PAIR, 2 * rows, PAIR),
            bf16(half // HEAD_DIM, groups * rows, PAIR),
            bf16(half // HEAD_DIM, groups * rows, PAIR),
            f32(half // HEAD_DIM, 2 * rows, PAIR),
            bf16(rows, half), bf16(2, rows, half),
            bf16(*pieces.shape), bf16(*pieces.shape), bf16(groups, *pieces.shape),
            bf16(HEADS // 2, rows, PAIR), bf16(keys, 2 * D), f32(rows, D), bf16(rows, D),
            chunk_sem, dma((2,)), dma, dma((7,)),
            chunk_sem, chunk_sem, chunk_sem, chunk_sem, chunk_sem, chunk_sem, dma, dma,
            slot_sem, slot_sem, slot_sem, slot_sem, dma((3,)), dma((3,)),
        ],
        compiler_params=pltpu.CompilerParams(
            collective_id=0, has_side_effects=True, vmem_limit_bytes=60 << 20),
        cost_estimate=pl.CostEstimate(
            flops=20 * 10 ** 9, bytes_accessed=16 << 20, transcendentals=21 * 10 ** 6),
    )(
        owner, eq_len, tokens, norm_gain.reshape(1, D), cross_gain.reshape(1, D), pieces,
        w_qkv, w_out, w_cq, w_ckv, w_cout,
    )
    return joined[None]


def solution(mesh):
    split = P("dp", "seq", None)
    in_specs = (split, split) + (P(),) * 9
    return jax.shard_map(
        per_device, mesh=mesh, in_specs=in_specs, out_specs=split, check_vma=False
    )
```

```python
import math
import jax
import jax.numpy as jnp
from jax import lax
from jax.experimental import pallas as pl
from jax.experimental.pallas import tpu as pltpu
from jax.sharding import PartitionSpec as P

D = 1024
HEADS = 16
HEAD_DIM = 64
PAIR = 2 * HEAD_DIM
Q_SCALE = math.log2(math.e) * HEAD_DIM ** (-0.5)
V_SHRINK = 2.0 ** -10
V_GROW = 2.0 ** 10
CHUNKS = 2
EXTRA = 16
MESH = pl.DeviceIdType.MESH


def rms(values, gain):
    return values * lax.rsqrt(jnp.mean(values * values, axis=-1, keepdims=True) + 1e-06) * gain


def dot(a, b):
    return jnp.dot(a, b, preferred_element_type=jnp.float32)


def dot_nt(a, b):
    return lax.dot_general(a, b, (((1,), (1,)), ((), ())), preferred_element_type=jnp.float32)


def low_lanes(rows):
    return lax.broadcasted_iota(jnp.int32, (rows, PAIR), 1) < HEAD_DIM


def finish(even, odd, low):
    total = pltpu.roll(jnp.where(low, odd, even), HEAD_DIM, axis=1)
    return (jnp.where(low, even, odd) * (V_GROW / total)).astype(jnp.bfloat16)


def kernel(
    owner_ref, len_ref, x_hbm, gain_hbm, cross_gain_hbm, eq_hbm,
    w_hbm, wo_hbm, wq_hbm, wkv_hbm, wc_hbm, out_ref,
    x_ref, gains, eq_ref, wbuf, wo, wq, wkv, wc,
    xn, q_s, k_s, v_s, acc, away, att, got, picked, eq_out, cross_q, kv_s, mixed, cross_att,
    x_sem, g_sem, e_sem, w_sem,
    part_send, part_recv, sib_send, sib_recv, fwd_send, fwd_recv, att_send, att_recv,
    one_send, one_recv, two_send, two_recv, eq_send, eq_recv,
):
    slots = eq_ref.shape[0]
    my_dp = lax.axis_index("dp")
    me = lax.axis_index("seq")
    core = lax.rem(me, 2)
    sib = me + 1 - 2 * core
    part = lax.rem(me + 2, 4)
    rows = x_ref.shape[0]
    half = D // 2
    pairs = half // PAIR
    step = rows // CHUNKS
    groups = xn.shape[0]

    def load(src, dst, sem):
        copy = pltpu.make_async_copy(src, dst, sem)
        copy.start()
        return copy

    x_loads = []
    for i in range(CHUNKS):
        here = pl.ds(i * step, step)
        x_loads.append(load(x_hbm.at[here], x_ref.at[here], x_sem.at[i]))
        if i == 0:
            gain_load = load(gain_hbm, gains.at[0], g_sem.at[0])
    eq_load = load(eq_hbm, eq_ref, e_sem)
    w_loads = []
    for j in range(3):
        cols = pl.ds(pl.multiple_of(core * half + j * D, half), half)
        w_loads.append(load(w_hbm.at[:, cols], wbuf.at[j], w_sem.at[j]))
    cross_gain_load = load(cross_gain_hbm, gains.at[1], g_sem.at[1])
    late = [
        load(src, dst, w_sem.at[3 + j])
        for j, (src, dst) in enumerate(((wkv_hbm, wkv), (wo_hbm, wo), (wq_hbm, wq), (wc_hbm, wc)))
    ]

    barrier = pltpu.get_barrier_semaphore()
    for other in (sib, part):
        pl.semaphore_signal(barrier, inc=1, device_id={"seq": other}, device_id_type=MESH)

    @pl.loop(1, slots)
    def _(i):
        peer = lax.rem(my_dp + i, slots)
        pl.semaphore_signal(barrier, inc=1, device_id={"dp": peer}, device_id_type=MESH)

    def scatter(i):
        peer = lax.rem(my_dp + i, slots)
        return pltpu.make_async_remote_copy(
            src_ref=eq_ref.at[peer], dst_ref=got.at[my_dp],
            send_sem=one_send.at[i], recv_sem=one_recv.at[i],
            device_id={"dp": peer}, device_id_type=MESH)

    def deliver(i):
        peer = lax.rem(my_dp + i, slots)
        return pltpu.make_async_remote_copy(
            src_ref=picked.at[i], dst_ref=eq_out.at[me, my_dp],
            send_sem=two_send.at[i], recv_sem=two_recv.at[i],
            device_id={"dp": peer}, device_id_type=MESH)

    def push(src, dst, send, recv, other):
        copy = pltpu.make_async_remote_copy(
            src_ref=src, dst_ref=dst, send_sem=send, recv_sem=recv,
            device_id={"seq": other}, device_id_type=MESH)
        copy.start()
        return copy

    gain_load.wait()
    gain = gains[0]
    to_part, to_sib = [], []
    for i in range(CHUNKS):
        here = pl.ds(i * step, step)
        x_loads[i].wait()
        xn[0, here] = rms(x_ref[here].astype(jnp.float32), gain).astype(jnp.bfloat16)
        if i == 0:
            pl.semaphore_wait(barrier, slots + 1)
        to_part.append(
            push(xn.at[0, here], xn.at[2, here], part_send.at[i], part_recv.at[i], part))
        to_sib.append(
            push(xn.at[0, here], xn.at[1, here], sib_send.at[i], sib_recv.at[i], sib))
    eq_load.wait()

    @pl.loop(1, slots)
    def _(i):
        scatter(i).start()

    got[my_dp] = eq_ref[my_dp]
    for copy in w_loads:
        copy.wait()

    low = low_lanes(step)

    def project(slot, i, with_q):
        at = pl.ds(i * step, step)
        x = xn[slot, at]
        start = slot * rows + i * step if slot < 2 else 2 * (rows + i * step) + (slot - 2) * step
        key_at = pl.ds(start, step)
        if with_q:
            qf = (dot(x, wbuf[0]) * Q_SCALE).astype(jnp.bfloat16)
            for p in range(pairs):
                q_s[p, key_at] = qf[:, p * PAIR:(p + 1) * PAIR]
        kf = dot(x, wbuf[1])
        vt = jnp.transpose(dot(x, wbuf[2]) * V_SHRINK).astype(jnp.bfloat16)
        for p in range(pairs):
            kp = kf[:, p * PAIR:(p + 1) * PAIR]
            k_s[2 * p, key_at] = jnp.where(low, kp, 0.0).astype(jnp.bfloat16)
            k_s[2 * p + 1, key_at] = jnp.where(low, 0.0, kp).astype(jnp.bfloat16)
        for h in range(2 * pairs):
            v_s[h, :HEAD_DIM, key_at] = vt[h * HEAD_DIM:(h + 1) * HEAD_DIM]

    def piece(p, h, key_at):
        w = jnp.exp2(dot_nt(k_s[2 * p + h, key_at], q_s[p])).astype(jnp.bfloat16)
        return dot(v_s[2 * p + h, :, key_at], w)

    for h in range(2 * pairs):
        v_s[h, HEAD_DIM:] = jnp.ones((EXTRA, groups * rows), jnp.bfloat16)
    for i in range(CHUNKS):
        project(0, i, True)

    @pl.loop(1, slots)
    def _(i):
        scatter(i).wait()

    @pl.loop(1, slots)
    def _(i):
        picked[i] = got[owner_ref[lax.rem(my_dp + i, slots)]]
        deliver(i).start()

    eq_out[me, my_dp] = got[owner_ref[my_dp]]
    for i in range(CHUNKS):
        to_sib[i].wait_recv()
        project(1, i, True)

    def local(p):
        for h in range(2):
            acc[2 * p + h] = piece(p, h, pl.ds(0, rows)) + piece(p, h, pl.ds(rows, rows))

    pl.loop(0, pairs // 2)(local)

    @pl.loop(1, slots)
    def _(i):
        deliver(i).wait()

    mine = eq_out.at[me]
    eq_part = push(mine, mine, eq_send.at[0], eq_recv.at[0], part)
    eq_sib = push(mine, mine, eq_send.at[1], eq_recv.at[1], sib)
    pl.loop(pairs // 2, pairs)(local)

    forwards = []
    for i in range(CHUNKS):
        here = pl.ds(i * step, step)
        to_part[i].wait_recv()
        forwards.append(
            push(xn.at[2, here], xn.at[3, here], fwd_send.at[i], fwd_recv.at[i], sib))
        for slot in (2, 3):
            if slot == 3:
                if i == CHUNKS - 1:
                    eq_part.wait_recv()
                    theirs = eq_out.at[part]
                    eq_fwd = push(theirs, theirs, eq_send.at[2], eq_recv.at[2], sib)
                forwards[i].wait_recv()
            project(slot, i, False)
        key_at = pl.ds(2 * (rows + i * step), 2 * step)

        @pl.loop(0, pairs)
        def _(p):
            for h in range(2):
                acc[2 * p + h] += piece(p, h, key_at)

    qlow = low_lanes(rows)

    def last(p, q_at):
        parts = []
        for h in range(2):
            total = acc[2 * p + h, HEAD_DIM:HEAD_DIM + 1, q_at]
            parts.append(acc[2 * p + h, :HEAD_DIM, q_at] * (V_GROW / total))
        return jnp.transpose(jnp.concatenate(parts, axis=0)).astype(jnp.bfloat16)

    for p in range(pairs):
        away[:, p * PAIR:(p + 1) * PAIR] = last(p, pl.ds(rows, rows))
    back = push(away, att.at[core], att_send, att_recv, sib)
    for p in range(pairs):
        att[core, :, p * PAIR:(p + 1) * PAIR] = last(p, pl.ds(0, rows))

    eq_part.wait_send()
    eq_sib.wait()
    eq_fwd.wait()
    cross_gain_load.wait()
    for copy in late:
        copy.wait()
    keys = kv_s.shape[0]
    equation = eq_out[...].reshape(keys, D)
    for j in range(4):
        cols = slice(j * half, (j + 1) * half)
        kv_s[:, cols] = dot(equation, wkv[:, cols]).astype(jnp.bfloat16)
    back.wait()
    for copy in to_part + to_sib + forwards:
        copy.wait_send()

    @pl.loop(0, CHUNKS)
    def _(r):
        at = pl.ds(pl.multiple_of(r * step, step), step)
        m = (x_ref[at].astype(jnp.float32)
             + dot(att[0, at], wo[:half]) + dot(att[1, at], wo[half:]))
        mixed[at] = m
        cross_in = rms(m, gains[1]).astype(jnp.bfloat16)
        qf = (dot(cross_in, wq[...]) * Q_SCALE).astype(jnp.bfloat16)
        for p in range(HEADS // 2):
            cross_q[p, at] = qf[:, p * PAIR:(p + 1) * PAIR]

    length = len_ref[owner_ref[my_dp]]
    klow = low_lanes(keys)
    valid = lax.broadcasted_iota(jnp.int32, (keys, PAIR), 0) < length
    one = jnp.where(valid, 1.0, 0.0)
    for p in range(HEADS // 2):
        cols = slice(p * PAIR, (p + 1) * PAIR)
        kp = jnp.where(valid, kv_s[:, cols].astype(jnp.float32), 0.0)
        vp = jnp.where(valid, kv_s[:, D + p * PAIR:D + (p + 1) * PAIR].astype(jnp.float32), 0.0)
        vp = vp * V_SHRINK
        outs = []
        for h in range(2):
            own = klow if h == 0 else jnp.logical_not(klow)
            kh = jnp.where(own, kp, 0.0).astype(jnp.bfloat16)
            vh = jnp.where(own, vp, one).astype(jnp.bfloat16)
            w = jnp.exp2(dot_nt(cross_q[p], kh)).astype(jnp.bfloat16)
            outs.append(dot(w, vh))
        cross_att[:, cols] = finish(outs[0], outs[1], qlow)

    @pl.loop(0, CHUNKS)
    def _(r):
        at = pl.ds(pl.multiple_of(r * step, step), step)
        out_ref[at] = (mixed[at] + dot(cross_att[at], wc[...])).astype(jnp.bfloat16)


def per_device(
    field, eq_embed, eq_len, owner, norm_gain, w_qkv, w_out, cross_gain, w_cq, w_ckv, w_cout
):
    tokens = field[0]
    rows = tokens.shape[0]
    half = D // 2
    slots = owner.shape[0]
    pieces = eq_embed.reshape(slots, eq_embed.shape[1] // slots, D)
    groups = lax.axis_size("seq")
    keys = groups * eq_embed.shape[1]
    any_space = pl.BlockSpec(memory_space=pl.ANY)
    smem = pl.BlockSpec(memory_space=pltpu.SMEM)
    dma = pltpu.SemaphoreType.DMA
    bf16 = lambda *shape: pltpu.VMEM(shape, jnp.bfloat16)
    f32 = lambda *shape: pltpu.VMEM(shape, jnp.float32)
    chunk_sem = dma((CHUNKS,))
    slot_sem = dma((slots,))
    joined = pl.pallas_call(
        kernel,
        name="joining_layer",
        out_shape=jax.ShapeDtypeStruct((rows, D), jnp.bfloat16),
        in_specs=[smem] * 2 + [any_space] * 9,
        out_specs=pl.BlockSpec(memory_space=pltpu.VMEM),
        scratch_shapes=[
            bf16(rows, D), f32(2, 1, D), bf16(*pieces.shape), bf16(3, D, half),
            bf16(D, D), bf16(D, D), bf16(D, 2 * D), bf16(D, D),
            bf16(groups, rows, D),
            bf16(half // PAIR, 2 * rows, PAIR),
            bf16(half // HEAD_DIM, groups * rows, PAIR),
            bf16(half // HEAD_DIM, HEAD_DIM + EXTRA, groups * rows),
            f32(half // HEAD_DIM, HEAD_DIM + EXTRA, 2 * rows),
            bf16(rows, half), bf16(2, rows, half),
            bf16(*pieces.shape), bf16(*pieces.shape), bf16(groups, *pieces.shape),
            bf16(HEADS // 2, rows, PAIR), bf16(keys, 2 * D), f32(rows, D), bf16(rows, D),
            chunk_sem, dma((2,)), dma, dma((7,)),
            chunk_sem, chunk_sem, chunk_sem, chunk_sem, chunk_sem, chunk_sem, dma, dma,
            slot_sem, slot_sem, slot_sem, slot_sem, dma((3,)), dma((3,)),
        ],
        compiler_params=pltpu.CompilerParams(
            collective_id=0, has_side_effects=True, vmem_limit_bytes=60 << 20),
        cost_estimate=pl.CostEstimate(
            flops=20 * 10 ** 9, bytes_accessed=16 << 20, transcendentals=21 * 10 ** 6),
    )(
        owner, eq_len, tokens, norm_gain.reshape(1, D), cross_gain.reshape(1, D), pieces,
        w_qkv, w_out, w_cq, w_ckv, w_cout,
    )
    return joined[None]


def solution(mesh):
    split = P("dp", "seq", None)
    in_specs = (split, split) + (P(),) * 9
    return jax.shard_map(
        per_device, mesh=mesh, in_specs=in_specs, out_specs=split, check_vma=False
    )
```
